256 devices in a mesh: seq: 4 (over y), ctx: 8 (over z_lo, core), head: 8 (over x, z_hi).
Axes of the slice: x: 4, y: 4, z: 8 (z_hi: 2, z_lo: 4; z = z_hi * 4 + z_lo), core: 2. Of those that a mesh axis runs over, the one named last changes fastest.
Arguments:
- queries: bfloat16 [4, 2, 2048, 4096], P('seq', None, 'ctx', 'head'), may hold values from -8 to 8
- key_vectors: bfloat16 [4, 2, 2048, 4096], P('seq', None, 'ctx', 'head'), may hold values from -8 to 8
- value_vectors: bfloat16 [4, 2, 2048, 4096], P('seq', None, 'ctx', 'head'), may hold values from -6 to 6
- token_rates: float32 [4, 2, 2048, 16], P('seq', None, 'ctx', 'head'), may hold values from 0.003 to 0.03
- fast_in: bfloat16 [16, 256, 512], P('head'), may hold values from -0.375 to 0.375
- fast_gate: bfloat16 [16, 256, 512], P('head'), may hold values from -0.375 to 0.375
- fast_out: bfloat16 [16, 512, 256], P('head'), may hold values from -0.25 to 0.25
- out_gain: float32 [4096], P('head'), may hold values from 0.1 to 1.9
- out_weight: bfloat16 [4096, 4096], P('head'), may hold values from -0.09375 to 0.09375
- cotangent: bfloat16 [4, 2, 2048, 4096], P('seq', None, 'ctx', 'head'), may hold values from -6 to 6
Outputs:
- layer_out: bfloat16 [4, 2, 2048, 4096], P('seq', None, 'ctx', 'head')
- weight_grad: float32 [4096, 4096], P('head', ('seq', 'ctx'))
- final_in: float32 [4, 16, 256, 512], P('seq', 'head')
- final_gate: float32 [4, 16, 256, 512], P('seq', 'head')
- final_out: float32 [4, 16, 512, 256], P('seq', 'head')
The draws below stay inside these ranges and needn't reach their ends.
All inputs are finite; a program needn't handle non-finite values.
Results may differ from the reference program's by a relative error of at most 0.024.
Values may be sent and summed in bfloat16 or wider, within the bound.
No kernel may reach another device: no remote copies, remote signals or barrier semaphores. Data moves between devices by JAX's collectives and lax.ppermute only.
A program may use at most 128 MiB of HBM per device.

```python
import math
import jax
import jax.numpy as jnp
from jax import lax

DH = 256
FH = 512
NCH = 2
SEQS = 4
GROUP = 2048
WIN = 256
HEADS = 16
D = 4096


def drawn_pair(key):
    full_shape = (SEQS, NCH, GROUP, D)
    drawn_query = jnp.clip(jax.random.normal(jax.random.fold_in(key, 101), full_shape, jnp.float32), -6.0, 6.0)
    drawn_keys = jnp.clip(jax.random.normal(jax.random.fold_in(key, 102), full_shape, jnp.float32), -6.0, 6.0)
    return (drawn_query, drawn_keys)


def draw_queries(key, part):
    return drawn_pair(key)[0].astype(jnp.bfloat16)


def draw_key_vectors(key, part):
    return drawn_pair(key)[1].astype(jnp.bfloat16)


def with_spikes(result, stream_key, source, target, parts, factor):
    owner, partner = [(jnp.arange(result.shape[axis_at]) // (result.shape[axis_at] // parts)).reshape([-1 if axis == axis_at else 1 for axis in range(result.ndim)]) for axis_at in (source, target)]
    chosen = jax.random.permutation(stream_key, parts)[partner]
    strong = (owner == chosen) | (owner == (partner + parts // 2) % parts)
    return jnp.where(strong, factor * result, result)


def levels(rng, shape, shards, least, high):
    gain = 1.0
    for axis_at, blocks in shards:
        heights = jax.random.uniform(jax.random.fold_in(jax.random.fold_in(rng, 6), axis_at), (blocks,), jnp.float32, least / len(shards), high / len(shards))
        gain = gain * jnp.repeat(jnp.exp(heights), shape[axis_at] // blocks).reshape((-1,) + (1,) * (len(shape) - 1 - axis_at))
    return gain


def normal_values(key, dims, width, reach, split=(), kind=jnp.bfloat16):
    array = jax.random.normal(key, dims, jnp.float32) * width
    if len(split) > 0:
        array = levels(key, dims, split, -0.22, 0.18) * array
    return jnp.clip(array, min=-reach, max=reach).astype(kind)


def noise_with(stream_key, dims, spread, limit, cuts, heavy, kind=jnp.bfloat16):
    values = spread * jax.random.normal(stream_key, dims, jnp.float32)
    if cuts:
        values = values * levels(stream_key, dims, cuts, -0.22, 0.18)
    return jnp.clip(with_spikes(values, jax.random.fold_in(stream_key, 3), *heavy), -limit, limit).astype(kind)


def setup_inputs(seed: int = 0) -> dict:
    key_list = jax.random.split(jax.random.key(seed), 11)
    return {
        "queries": draw_queries(jax.random.fold_in(key_list[10], 71), 0),
        "key_vectors": draw_key_vectors(jax.random.fold_in(key_list[10], 71), 0),
        "value_vectors": normal_values(key_list[2], (SEQS, NCH, GROUP, D), 1.0, 6.0, ((0, 4), (2, 8), (3, 8))),
        "token_rates": jnp.clip(jnp.exp(math.log(0.03) - 2.3025851 * jax.random.uniform(key_list[3], (SEQS, NCH, GROUP, HEADS), jnp.float32) ** levels(key_list[3], (SEQS, NCH, GROUP, HEADS), ((0, 4), (2, 8), (3, 8)), -0.2, 0.2)), 0.003, 0.03),
        "fast_in": normal_values(key_list[4], (HEADS, DH, FH), DH ** -0.5, 0.375, ((0, 8),)),
        "fast_gate": normal_values(key_list[5], (HEADS, DH, FH), DH ** -0.5, 0.375, ((0, 8),)),
        "fast_out": normal_values(key_list[6], (HEADS, FH, DH), FH ** -0.5, 0.25, ((0, 8),)),
        "out_gain": jnp.clip(1.0 + 0.18 * jax.random.normal(key_list[7], (D,), jnp.float32), 0.1, 1.9),
        "out_weight": normal_values(key_list[8], (D, D), D ** -0.5, 0.09375, ((0, 8),)),
        "cotangent": noise_with(key_list[9], (SEQS, NCH, GROUP, D), 1.0, 6.0, ((0, 4), (2, 8), (3, 8)), (2, 3, 8, 2.0)),
    }


def normalize_rms(values_in, epsilon):
    return values_in * lax.rsqrt(lax.optimization_barrier(jnp.mean(values_in * values_in, axis=-1, keepdims=True)) + epsilon)

def column_norms(weight):
    return jnp.sqrt(lax.optimization_barrier(jnp.sum(weight * weight, axis=-2, keepdims=True)) + 1e-06)

def renorm(weight, target):
    return weight * (target / jnp.sqrt(lax.optimization_barrier(jnp.sum(weight * weight, axis=-2, keepdims=True)) + 1e-06))

def fast_head(head_in, head_gate, head_out, query_head, key_head, value_head, rate_head):
    weight_in = head_in.astype(jnp.float32)
    weight_gate = head_gate.astype(jnp.float32)
    weight_out = head_out.astype(jnp.float32)
    target_in = column_norms(weight_in)
    target_gate = column_norms(weight_gate)
    target_out = column_norms(weight_out)
    results = []
    for block_index in range(NCH):
        query_norm = normalize_rms(query_head[block_index].astype(jnp.float32), 1e-05).astype(jnp.bfloat16)
        key_norm = normalize_rms(key_head[block_index].astype(jnp.float32), 1e-05).astype(jnp.bfloat16)
        round_in = weight_in.astype(jnp.bfloat16)
        round_gate = weight_gate.astype(jnp.bfloat16)
        round_out = weight_out.astype(jnp.bfloat16)
        hidden = (jax.nn.silu(jnp.dot(query_norm, round_in, preferred_element_type=jnp.float32)) * jnp.dot(query_norm, round_gate, preferred_element_type=jnp.float32)).astype(jnp.bfloat16)
        results.append(jnp.dot(hidden, round_out, preferred_element_type=jnp.float32))
        key_in = jnp.dot(key_norm, round_in, preferred_element_type=jnp.float32)
        key_gate = jnp.dot(key_norm, round_gate, preferred_element_type=jnp.float32)
        sigmoid_in = jax.nn.sigmoid(key_in)
        active = key_in * sigmoid_in
        feature = (active * key_gate).astype(jnp.bfloat16)
        scaled_values = (rate_head[block_index][:, None] * value_head[block_index].astype(jnp.float32)).astype(jnp.bfloat16)
        d_feature = jnp.dot(scaled_values, round_out.T, preferred_element_type=jnp.float32)
        d_in = (d_feature * key_gate * sigmoid_in * (1.0 + key_in * (1.0 - sigmoid_in))).astype(jnp.bfloat16)
        d_gate = (d_feature * active).astype(jnp.bfloat16)
        weight_in = renorm(weight_in + jnp.dot(key_norm.T, d_in, preferred_element_type=jnp.float32), target_in)
        weight_gate = renorm(weight_gate + jnp.dot(key_norm.T, d_gate, preferred_element_type=jnp.float32), target_gate)
        weight_out = renorm(weight_out + jnp.dot(feature.T, scaled_values, preferred_element_type=jnp.float32), target_out)
    return (jnp.stack(results), weight_in, weight_gate, weight_out)

def window_attention(query_seq, key_seq, value_seq):
    length = query_seq.shape[0]
    blocks = length // WIN
    padded_keys = jnp.concatenate([jnp.zeros((WIN,) + key_seq.shape[1:], key_seq.dtype), key_seq], axis=0)
    padded_values = jnp.concatenate([jnp.zeros((WIN,) + value_seq.shape[1:], value_seq.dtype), value_seq], axis=0)
    score_scale = 1.0 / math.sqrt(DH)
    query_pos = jnp.arange(WIN, dtype=jnp.int32)[:, None]
    key_pos = jnp.arange(2 * WIN, dtype=jnp.int32)[None, :]

    def attend_block(block_number):
        start_row = (block_number * WIN).astype(jnp.int32)
        query_block = lax.dynamic_slice_in_dim(query_seq, start_row, WIN, 0).astype(jnp.float32)
        key_block = lax.dynamic_slice_in_dim(padded_keys, start_row, 2 * WIN, 0).astype(jnp.float32)
        value_block = lax.dynamic_slice_in_dim(padded_values, start_row, 2 * WIN, 0).astype(jnp.float32)
        scores = jnp.einsum('qhd,khd->hqk', query_block, key_block) * score_scale
        allowed = (key_pos > query_pos) & (key_pos <= query_pos + WIN) & (start_row + key_pos >= WIN)
        scores = jnp.where(allowed[None], scores, -jnp.inf)
        largest = lax.optimization_barrier(jnp.max(scores, axis=-1, keepdims=True))
        powers = jnp.exp(scores - largest)
        attn_weights = (powers / lax.optimization_barrier(jnp.sum(powers, axis=-1, keepdims=True))).astype(jnp.bfloat16)
        return jnp.einsum('hqk,khd->qhd', attn_weights.astype(jnp.float32), value_block)
    results = lax.map(attend_block, jnp.arange(blocks, dtype=jnp.int32))
    return results.reshape(length, HEADS, DH)

def reference(queries, key_vectors, value_vectors, token_rates, fast_in, fast_gate, fast_out, out_gain, out_weight, cotangent):
    length = NCH * GROUP
    mixed_list = []
    final_ins = []
    final_gates = []
    final_outs = []
    grad_total = jnp.zeros((D, D), jnp.float32)
    for sequence in range(SEQS):
        query_heads = jnp.moveaxis(queries[sequence].reshape(NCH, GROUP, HEADS, DH), 2, 0)
        key_heads = jnp.moveaxis(key_vectors[sequence].reshape(NCH, GROUP, HEADS, DH), 2, 0)
        value_heads = jnp.moveaxis(value_vectors[sequence].reshape(NCH, GROUP, HEADS, DH), 2, 0)
        rate_heads = jnp.moveaxis(token_rates[sequence], 2, 0)
        fast_result, final_one, final_two, final_three = lax.map(lambda packed: fast_head(*packed), (fast_in, fast_gate, fast_out, query_heads, key_heads, value_heads, rate_heads))
        fast_flat = jnp.moveaxis(fast_result, 0, 2).reshape(length, HEADS, DH)
        attended = window_attention(queries[sequence].reshape(length, HEADS, DH), key_vectors[sequence].reshape(length, HEADS, DH), value_vectors[sequence].reshape(length, HEADS, DH))
        combined = (normalize_rms(fast_flat, 1e-05) * out_gain.reshape(HEADS, DH) + attended).astype(jnp.bfloat16).reshape(length, D)
        mixed_list.append(jnp.dot(combined, out_weight, preferred_element_type=jnp.float32).astype(jnp.bfloat16).reshape(NCH, GROUP, D))
        grad_total = grad_total + jnp.dot(combined.T, cotangent[sequence].reshape(length, D), preferred_element_type=jnp.float32)
        final_ins.append(final_one)
        final_gates.append(final_two)
        final_outs.append(final_three)
    return (jnp.stack(mixed_list), grad_total, jnp.stack(final_ins), jnp.stack(final_gates), jnp.stack(final_outs))
```

```python
import functools
import math

import jax
import jax.numpy as jnp
from jax import lax
from jax.experimental import pallas as pl
from jax.experimental.pallas import tpu as pltpu
from jax.sharding import PartitionSpec as P

F32 = jnp.float32
BF16 = jnp.bfloat16


def permuted(value, axis, target):
    count = lax.axis_size(axis)
    return lax.ppermute(value, axis, [(source, target(source)) for source in range(count)])


def over_core(value):
    return permuted(value, "ctx", lambda i: i ^ 1)


def over_line(value, step):
    return permuted(value, "ctx", lambda i: i ^ (2 * step))


def over_x(value, step):
    return permuted(value, "head", lambda i: i ^ (2 * step))


def over_z_half(value):
    return permuted(value, "head", lambda i: i ^ 1)


def over_y(value, step):
    return permuted(value, "seq", lambda i: i ^ step)


def kernel_call(body, name, *, ids, args, outs, scratch=(), flops=0):
    size = sum(a.size * a.dtype.itemsize for a in args)
    size += sum(math.prod(s) * jnp.dtype(d).itemsize for s, d in outs)
    return pl.pallas_call(
        body,
        name=name,
        out_shape=[jax.ShapeDtypeStruct(s, d) for s, d in outs],
        in_specs=[pl.BlockSpec(memory_space=pltpu.SMEM)]
        + [pl.BlockSpec(memory_space=pltpu.VMEM)] * len(args),
        out_specs=[pl.BlockSpec(memory_space=pltpu.VMEM)] * len(outs),
        scratch_shapes=list(scratch),
        cost_estimate=pl.CostEstimate(flops=flops, bytes_accessed=size, transcendentals=0),
    )(ids, *args)


def dot(a, b):
    return lax.dot_general(a, b, (((1,), (0,)), ((), ())), preferred_element_type=F32)


def dot_nt(a, b):
    return lax.dot_general(a, b, (((1,), (1,)), ((), ())), preferred_element_type=F32)


def dot_tn(a, b):
    return lax.dot_general(a, b, (((0,), (0,)), ((), ())), preferred_element_type=F32)


def normalize_rms(values, epsilon):
    return values * lax.rsqrt(jnp.mean(values * values, axis=-1, keepdims=True) + epsilon)


def sigmoid(a):
    return 1.0 / (1.0 + jnp.exp(-a))


def prepare_body(ids, fin, fgate, fout, wi, wg, wot, shard):
    line, core = ids[0], ids[1]
    wi[...] = fin[core]
    wg[...] = fgate[core]
    wot[...] = fout[core].astype(F32).T.astype(BF16)
    column = pl.ds(pl.multiple_of(line * 128, 128), 128)
    shard[0:256, :] = wi[:, column].astype(F32)
    shard[256:512, :] = wg[:, column].astype(F32)
    rows = wot[pl.ds(pl.multiple_of(line * 64, 64), 64), :].astype(F32)
    for c in range(4):
        shard[512 + 64 * c : 576 + 64 * c, :] = rows[:, 128 * c : 128 * c + 128]


def update_body(ids, k0, k1, s0, s1, wi, wg, wot, o0, o1, o2, o3, ui, ug, uo):
    line = ids[0]
    for part, (k, s) in enumerate(((k0, s0), (k1, s1))):
        key_norm = normalize_rms(k[...].astype(F32), 1e-05).astype(BF16)
        scaled = s[...]
        key_in = dot(key_norm, wi[...])
        key_gate = dot(key_norm, wg[...])
        d_feature = dot(scaled, wot[...])
        sig = sigmoid(key_in)
        active = key_in * sig
        feature = (active * key_gate).astype(BF16)
        d_in = (d_feature * key_gate * sig * (1.0 + key_in * (1.0 - sig))).astype(BF16)
        d_gate = (d_feature * active).astype(BF16)
        if part == 0:
            ui[...] = dot_tn(key_norm, d_in)
            ug[...] = dot_tn(key_norm, d_gate)
            uo[...] = dot_tn(scaled, feature)
        else:
            ui[...] += dot_tn(key_norm, d_in)
            ug[...] += dot_tn(key_norm, d_gate)
            uo[...] += dot_tn(scaled, feature)
    for step, out in enumerate((o0, o1, o2, o3)):
        owner = line ^ step
        column = pl.ds(pl.multiple_of(owner * 128, 128), 128)
        out[0:256, :] = ui[:, column].astype(out.dtype)
        out[256:512, :] = ug[:, column].astype(out.dtype)
        rows = uo[pl.ds(pl.multiple_of(owner * 64, 64), 64), :].astype(out.dtype)
        for c in range(4):
            out[512 + 64 * c : 576 + 64 * c, :] = rows[:, 128 * c : 128 * c + 128]


def renorm_body(ids, first, current, own, r1, r2, r3, new, rounded):
    total = (
        current[...]
        + own[...]
        + r1[...].astype(F32)
        + r2[...].astype(F32)
        + r3[...].astype(F32)
    )
    start = first[...]
    for low in (0, 256):
        w0, w = start[low : low + 256], total[low : low + 256]
        target = jnp.sqrt(jnp.sum(w0 * w0, axis=0, keepdims=True) + 1e-06)
        scale = target / jnp.sqrt(jnp.sum(w * w, axis=0, keepdims=True) + 1e-06)
        value = w * scale
        new[low : low + 256, :] = value
        rounded[low : low + 256, :] = value.astype(BF16)
    parts = [slice(512 + 64 * c, 576 + 64 * c) for c in range(4)]
    sum0 = sum(jnp.sum(start[p] * start[p], axis=1, keepdims=True) for p in parts)
    sum1 = sum(jnp.sum(total[p] * total[p], axis=1, keepdims=True) for p in parts)
    scale = jnp.sqrt(sum0 + 1e-06) / jnp.sqrt(sum1 + 1e-06)
    for p in parts:
        value = total[p] * scale
        new[p, :] = value
        rounded[p, :] = value.astype(BF16)


def unpack_body(ids, p0, p1, p2, p3, wi, wg, wot):
    line = ids[0]
    for step, piece in enumerate((p0, p1, p2, p3)):
        owner = line ^ step
        column = pl.ds(pl.multiple_of(owner * 128, 128), 128)
        wi[:, column] = piece[0:256, :]
        wg[:, column] = piece[256:512, :]
        for c in range(4):
            wot[pl.ds(pl.multiple_of(owner * 64, 64), 64), 128 * c : 128 * c + 128] = piece[
                512 + 64 * c : 576 + 64 * c, :
            ]


def final_body(ids, p0, p1, p2, p3, q0, q1, q2, q3, fin, fgate, fout, wot):
    line, core = ids[0], ids[1]
    for head, pieces in ((core, (p0, p1, p2, p3)), (1 - core, (q0, q1, q2, q3))):
        for step, piece in enumerate(pieces):
            owner = line ^ step
            column = pl.ds(pl.multiple_of(owner * 128, 128), 128)
            fin[head, :, column] = piece[0:256, :].astype(F32)
            fgate[head, :, column] = piece[256:512, :].astype(F32)
            for c in range(4):
                wot[pl.ds(pl.multiple_of(owner * 64, 64), 64), 128 * c : 128 * c + 128] = piece[
                    512 + 64 * c : 576 + 64 * c, :
                ].astype(F32)
        fout[head] = wot[...].T


def attention_body(ids, q, k, v, rk, rv, out):
    line = ids[0]
    first = (line == 0).astype(jnp.int32)
    query_pos = lax.broadcasted_iota(jnp.int32, (256, 512), 0)
    key_pos = lax.broadcasted_iota(jnp.int32, (256, 512), 1)
    inside = (key_pos > query_pos) & (key_pos <= query_pos + 256)
    for block in range(2):
        source = 0 if block == 0 else 1 - first
        for tile in range(2):
            if tile == 0:
                keys = jnp.concatenate([rk[source], k[block, 0]], axis=0)
                vals = jnp.concatenate([rv[source], v[block, 0]], axis=0)
            else:
                keys = jnp.concatenate([k[block, 0], k[block, 1]], axis=0)
                vals = jnp.concatenate([v[block, 0], v[block, 1]], axis=0)
            allowed = inside
            if block == 0 and tile == 0:
                allowed = inside & (key_pos >= 256 * first)
            scores = dot_nt(q[block, tile], keys) * (1.0 / 16.0)
            scores = jnp.where(allowed, scores, -jnp.inf)
            powers = jnp.exp(scores - jnp.max(scores, axis=-1, keepdims=True))
            weights = (powers / jnp.sum(powers, axis=-1, keepdims=True)).astype(BF16)
            out[block, tile] = dot(weights, vals)


def combine_body(block, ids, q, attended, gain, wi, wg, wot, out):
    for tile in range(2):
        query_norm = normalize_rms(q[block, tile].astype(F32), 1e-05).astype(BF16)
        a = dot(query_norm, wi[...])
        hidden = (a * sigmoid(a) * dot(query_norm, wg[...])).astype(BF16)
        fast = dot_nt(hidden, wot[...])
        value = normalize_rms(fast, 1e-05) * gain[...] + attended[block, tile]
        out[tile] = value.astype(BF16)


def project_body(ids, own, other, w, o0, o1, o2, o3):
    core, x = ids[1], ids[2]
    mine = pl.ds(pl.multiple_of(core * 256, 256), 256)
    theirs = pl.ds(pl.multiple_of((1 - core) * 256, 256), 256)
    a, b = own[core], other[core]
    for step, out in enumerate((o0, o1, o2, o3)):
        columns = pl.ds(pl.multiple_of((x ^ step) * 1024, 1024), 1024)
        out[...] = (dot(a, w[mine, columns]) + dot(b, w[theirs, columns])).astype(out.dtype)


def project_sum_body(ids, p0, p1, p2, p3, keep, send):
    half = ids[3]
    for owner, out in ((half, keep), (1 - half, send)):
        columns = pl.ds(pl.multiple_of(owner * 512, 512), 512)
        total = p0[:, columns].astype(F32) + p1[:, columns].astype(F32)
        total = total + p2[:, columns].astype(F32) + p3[:, columns].astype(F32)
        out[...] = total.astype(out.dtype)


def grad_body(ids, a0, a1, b0, b1, *rest):
    cots, out = rest[:8], rest[8]
    core, x, y = ids[1], ids[2], ids[4]
    for step in range(4):
        keep, got = cots[2 * step], cots[2 * step + 1]
        slot = step ^ x ^ y
        for head, (left0, left1) in ((core, (a0, a1)), (1 - core, (b0, b1))):
            total = dot_tn(left0[core], keep[0]) + dot_tn(left0[1 - core], got[0])
            total += dot_tn(left1[core], keep[1]) + dot_tn(left1[1 - core], got[1])
            out[slot, pl.ds(pl.multiple_of(head * 256, 256), 256), :] = total.astype(BF16)


def grad_sum_body(ids, p0, p1, p2, p3, o0, o1, o2, o3):
    line = ids[0]
    for step, out in enumerate((o0, o1, o2, o3)):
        columns = pl.ds(pl.multiple_of((line ^ step) * 128, 128), 128)
        total = p0[:, columns].astype(F32) + p1[:, columns].astype(F32)
        total = total + p2[:, columns].astype(F32) + p3[:, columns].astype(F32)
        out[...] = total.astype(BF16)


def line_target(step):
    def target(i):
        line, core = i // 2, i % 2
        return 4 * core + (line ^ step)

    return target


def shards(
    queries,
    key_vectors,
    value_vectors,
    token_rates,
    fast_in,
    fast_gate,
    fast_out,
    out_gain,
    out_weight,
    cotangent,
):
    ctx, head, y = lax.axis_index("ctx"), lax.axis_index("head"), lax.axis_index("seq")
    line, core, x, half = ctx // 2, ctx % 2, head // 2, head % 2
    ids = jnp.stack([line, core, x, half, y]).astype(jnp.int32)
    full = functools.partial(kernel_call, ids=ids)
    fat, thin = ((768, 128), F32), ((768, 128), BF16)
    wide = ((256, 512), BF16)

    def column_half(value, which):
        return lax.dynamic_slice_in_dim(value, which * 256, 256, axis=2)

    def absolute(own, other):
        return jnp.where(
            core == 0, jnp.stack([own, other], axis=1), jnp.stack([other, own], axis=1)
        )

    scaled = (
        token_rates[0][..., None] * value_vectors[0].reshape(2, 256, 2, 256).astype(F32)
    ).astype(BF16).reshape(2, 256, 512)
    mine, theirs = [], []
    for value in (key_vectors[0], scaled, value_vectors[0], queries[0]):
        mine.append(column_half(value, core))
        theirs.append(over_core(column_half(value, 1 - core)))
    gain = lax.dynamic_slice_in_dim(out_gain, core * 256, 256, 0).reshape(1, 256)

    wi, wg, wot, shard0 = full(
        prepare_body, "prepare", args=(fast_in, fast_gate, fast_out), outs=[wide] * 3 + [fat]
    )

    def reduced_update(block, weights, current):
        pieces = full(
            update_body,
            f"update{block}",
            args=(mine[0][block], theirs[0][block], mine[1][block], theirs[1][block], *weights),
            outs=[fat, thin, thin, thin],
            scratch=[pltpu.VMEM((256, 512), F32)] * 3,
            flops=2 * 6 * 512 * 256 * 512,
        )
        moved = [over_line(pieces[step], step) for step in (1, 2, 3)]
        new, rounded = full(
            renorm_body, f"renorm{block}", args=(shard0, current, pieces[0], *moved), outs=[fat, thin]
        )
        return new, [rounded] + [over_line(rounded, step) for step in (1, 2, 3)]

    weights0 = (wi, wg, wot)
    shard1, packed1 = reduced_update(0, weights0, shard0)
    weights1 = full(unpack_body, "unpack", args=packed1, outs=[wide] * 3)
    _, packed2 = reduced_update(1, weights1, shard1)
    partner2 = [over_core(piece) for piece in packed2]
    final_in, final_gate, final_out = full(
        final_body,
        "final",
        args=(*packed2, *partner2),
        outs=[((2, 256, 512), F32), ((2, 256, 512), F32), ((2, 512, 256), F32)],
        scratch=[pltpu.VMEM((256, 512), F32)],
    )

    keys, values, query = (absolute(mine[i], theirs[i]) for i in (0, 2, 3))
    rim_keys = over_line_next(keys[:, 1])
    rim_values = over_line_next(values[:, 1])
    (attended,) = full(
        attention_body,
        "attention",
        args=(query, keys, values, rim_keys, rim_values),
        outs=[((2, 2, 256, 256), F32)],
        flops=2 * 4 * 2 * 256 * 512 * 256,
    )

    combined, partner, outs = [], [], []
    for block, weights in ((0, weights0), (1, weights1)):
        (value,) = full(
            functools.partial(combine_body, block),
            f"combine{block}",
            args=(query, attended, gain, *weights),
            outs=[((2, 256, 256), BF16)],
            flops=2 * 3 * 512 * 256 * 512,
        )
        combined.append(value)
        partner.append(over_core(value))
        pieces = full(
            project_body,
            f"project{block}",
            args=(value, partner[block], out_weight),
            outs=[((256, 1024), BF16)] * 4,
            flops=2 * 256 * 512 * 4096,
        )
        moved = [over_x(pieces[step], step) for step in (1, 2, 3)]
        keep, send = full(
            project_sum_body,
            f"projectsum{block}",
            args=(pieces[0], *moved),
            outs=[((256, 512), F32), ((256, 512), BF16)],
        )
        outs.append((keep + over_z_half(send).astype(F32)).astype(BF16))
    layer_out = jnp.stack(outs)[None]

    own = cotangent[0]
    across = over_z_half(own)
    keep = jnp.where(half == core, own, across)
    got = over_core(jnp.where(half == core, across, own))
    cots = [keep, got]
    for step in (1, 2, 3):
        cots += [over_x(keep, step), over_x(got, step)]
    (grads,) = full(
        grad_body,
        "grad",
        args=(*combined, *partner, *cots),
        outs=[((4, 512, 512), BF16)],
        flops=2 * 1024 * 512 * 2048,
    )
    moved = [over_y(grads[step], step) for step in (1, 2, 3)]
    pieces = full(
        grad_sum_body, "gradsum", args=(grads[0], *moved), outs=[((512, 128), BF16)] * 4
    )
    arrived = [permuted(pieces[step], "ctx", line_target(step)) for step in range(4)]
    weight_grad = sum(piece.astype(F32) for piece in arrived)
    return (layer_out, weight_grad, final_in[None], final_gate[None], final_out[None])


def over_line_next(value):
    return permuted(value, "ctx", lambda i: (i + 2) % 8)


def solution(mesh):
    return jax.shard_map(
        shards,
        mesh=mesh,
        in_specs=(
            P("seq", None, "ctx", "head"),
            P("seq", None, "ctx", "head"),
            P("seq", None, "ctx", "head"),
            P("seq", None, "ctx", "head"),
            P("head", None, None),
            P("head", None, None),
            P("head", None, None),
            P("head"),
            P("head", None),
            P("seq", None, "ctx", "head"),
        ),
        out_specs=(
            P("seq", None, "ctx", "head"),
            P("head", ("seq", "ctx")),
            P("seq", "head", None, None),
            P("seq", "head", None, None),
            P("seq", "head", None, None),
        ),
        check_vma=False,
    )
```
